32 devices in a mesh: dp: 4 (over z), shard: 8 (over y, x, core).
Axes of the slice: x: 2, y: 2, z: 4, core: 2. Of those that a mesh axis runs over, the one named last changes fastest.
Arguments:
- attention_grad: float32 [4, 3968, 3968], P('dp', 'shard'), may hold values from -127 to 127
- attention_error: float32 [4, 3968, 3968], P('dp', 'shard'), may hold values from -64 to 64
- attention_warm: float32 [32, 3968], replicated, may hold values from -6 to 6
- feedforward_grad: float32 [4, 7936, 2048], P('dp', 'shard'), may hold values from -127 to 127
- feedforward_error: float32 [4, 7936, 2048], P('dp', 'shard'), may hold values from -64 to 64
- feedforward_warm: float32 [32, 2048], replicated, may hold values from -6 to 6
Outputs:
- attention_carry: float32 [4, 3968, 3968], P('dp', 'shard')
- feedforward_carry: float32 [4, 7936, 2048], P('dp', 'shard')
- attention_basis: float32 [32, 3968], replicated
- feedforward_basis: float32 [32, 2048], replicated
The draws below stay inside these ranges and needn't reach their ends.
All inputs are finite; a program needn't handle non-finite values.
Results may differ from the reference program's by a relative error of at most 0.00025.
Values sent between devices are 32-bit elements; how exact they have to be, the bound alone decides.
No kernel may reach another device: no remote copies, remote signals or barrier semaphores. Data moves between devices by JAX's collectives and lax.ppermute only.
A program may use at most 128 MiB of HBM per device.

```python
import jax
import jax.numpy as jnp
from jax import lax

D = 3968
FW = 7936
DW = 2048
R = 32
ITERS = 2
N_DP = 4


def scaled_field(key, replicas, rows, cols, amplitude):
    keys = jax.random.split(key, 3)
    position = jnp.arange(rows, dtype=jnp.float32) / rows
    row_scale = jnp.power(10.0, 0.5 * position + 0.5 * jax.random.uniform(keys[0], (rows,), jnp.float32))
    col_scale = jnp.power(10.0, jax.random.uniform(keys[1], (cols,), jnp.float32))
    replica_scale = jnp.power(10.0, 0.5 * jnp.arange(replicas, dtype=jnp.float32) / max(replicas - 1, 1))
    noise = jax.random.truncated_normal(keys[2], -4.0, 4.0, (replicas, rows, cols), jnp.float32)
    scale = replica_scale[:, None, None] * row_scale[None, :, None] * col_scale[None, None, :]
    return amplitude * noise * scale / 10.0


def draw_attention_grad(key, part):
    return scaled_field(jax.random.fold_in(key, 11), N_DP, D, D, 1.0)


def draw_attention_error(key, part):
    return scaled_field(jax.random.fold_in(key, 23), N_DP, D, D, 0.5)


def draw_feedforward_grad(key, part):
    return scaled_field(jax.random.fold_in(key, 37), N_DP, FW, DW, 1.0)


def draw_feedforward_error(key, part):
    return scaled_field(jax.random.fold_in(key, 41), N_DP, FW, DW, 0.5)


def scatter_about(stream_key, dims, scale, bound, kind=jnp.bfloat16):
    drawn = scale * jax.random.normal(stream_key, dims, jnp.float32)
    return jnp.clip(drawn, min=-bound, max=bound).astype(kind)


def setup_inputs(seed: int = 0) -> dict:
    seeds = jax.random.split(jax.random.key(seed), 7)
    return {
        "attention_grad": draw_attention_grad(jax.random.fold_in(seeds[6], 71), 0),
        "attention_error": draw_attention_error(jax.random.fold_in(seeds[6], 71), 0),
        "attention_warm": scatter_about(seeds[2], (R, D), 1.0, 6.0, jnp.float32),
        "feedforward_grad": draw_feedforward_grad(jax.random.fold_in(seeds[6], 71), 0),
        "feedforward_error": draw_feedforward_error(jax.random.fold_in(seeds[6], 71), 0),
        "feedforward_warm": scatter_about(seeds[5], (R, DW), 1.0, 6.0, jnp.float32),
    }


highest = lax.Precision.HIGHEST

def left_product(matrix, factor):
    return lax.dot_general(matrix.astype(jnp.float32), factor.astype(jnp.float32), (((1,), (1,)), ((), ())), precision=highest, preferred_element_type=jnp.float32)

def right_product(basis, matrix):
    return lax.dot_general(basis.astype(jnp.float32), matrix.astype(jnp.float32), (((0,), (0,)), ((), ())), precision=highest, preferred_element_type=jnp.float32)

def orthonormal(left, gram):
    lower = jnp.linalg.cholesky(gram)
    return jax.scipy.linalg.solve_triangular(lower, left.T, lower=True).T

def compress(gradient, feedback, factor):
    replicas = gradient.shape[0]
    rows = gradient.shape[1]
    basis = jnp.zeros((rows, factor.shape[0]), jnp.float32)
    for sweep in range(ITERS):
        current = factor

        def add_left(running, pieces):
            return (running + left_product(pieces[0] + pieces[1], current), None)
        left = lax.scan(add_left, jnp.zeros((rows, factor.shape[0]), jnp.float32), (gradient, feedback))[0]
        gram = right_product(left, left)
        basis = orthonormal(left, gram)

        def add_right(running, pieces):
            return (running + right_product(basis, pieces[0] + pieces[1]), None)
        summed = lax.scan(add_right, jnp.zeros(factor.shape, jnp.float32), (gradient, feedback))[0]
        factor = summed / replicas
    approx = jnp.dot(basis.astype(jnp.float32), factor.astype(jnp.float32), precision=highest, preferred_element_type=jnp.float32)
    carry = gradient + feedback - approx[None]
    return (carry, factor)

def reference(attention_grad, attention_error, attention_warm, feedforward_grad, feedforward_error, feedforward_warm):
    attention_carry, attention_basis = compress(attention_grad, attention_error, attention_warm)
    feedforward_carry, feedforward_basis = compress(feedforward_grad, feedforward_error, feedforward_warm)
    return (attention_carry, feedforward_carry, attention_basis, feedforward_basis)
```

```python
import functools

import jax
import jax.numpy as jnp
from jax import lax
from jax.experimental import pallas as pl
from jax.experimental.pallas import tpu as pltpu
from jax.sharding import PartitionSpec as P

ITERS = 2
LANES = 128
MIB = 1 << 20

highest = lax.Precision.HIGHEST
NT = (((1,), (1,)), ((), ()))
NN = (((1,), (0,)), ((), ()))
VMEM = pl.BlockSpec(memory_space=pltpu.VMEM)
ANY = pl.BlockSpec(memory_space=pl.ANY)


def dot(a, b, dims):
    return lax.dot_general(a, b, dims, preferred_element_type=jnp.float32)


def dot32(a, b, dims):
    return lax.dot_general(a, b, dims, precision=highest, preferred_element_type=jnp.float32)


def pad(n):
    return -(-n // LANES) * LANES


def split(x):
    high = x.astype(jnp.bfloat16)
    low = (x - high.astype(jnp.float32)).astype(jnp.bfloat16)
    return high, low


def stacked(x):
    high, low = split(x)
    return jnp.concatenate([high, low], axis=0)


def tree(terms):
    terms = list(terms)
    while len(terms) > 1:
        terms = [a + b for a, b in zip(terms[::2], terms[1::2])]
    return terms[0]


def three(pair, high, low, dims):
    rank = pair.shape[0] // 2
    first = dot(pair, high, dims)
    return first[:rank] + first[rank:] + dot(pair[:rank], low, dims)


class Plan:
    def __init__(self, rows, cols, rank, shards):
        self.rows, self.cols, self.rank, self.shards = rows, cols, rank, shards
        self.row_at = (0, pad(rows[0]))
        self.row_all = pad(rows[0]) + pad(rows[1])
        self.col_at = (0, pad(cols[0]))
        used = pad(cols[0]) + pad(cols[1])
        self.share = pad(-(-used // shards))
        self.col_all = self.share * shards


def slot_of(chunk, place, shards):
    offset = lax.bitwise_xor(jnp.int32(chunk), place)
    return (offset & 1) * (shards // 2) + (offset >> 1)


def load_kernel(plan, ag, ae, fg, fe, wa, wf, ha, la, hf, lf, pt, bufs, sems):
    pieces = []
    for m, (g, e, w, h, l) in enumerate(((ag, ae, wa, ha, la), (fg, fe, wf, hf, lf))):
        for r in range(0, plan.rows[m], LANES):
            pieces.append((m, r, min(LANES, plan.rows[m] - r), g, e, w, h, l))
    copies = []
    for i, (m, r, n, g, e, w, h, l) in enumerate(pieces):
        pair = []
        for j, src in enumerate((g, e)):
            pair.append(pltpu.make_async_copy(src.at[0, pl.ds(r, n)], bufs[2 * m + j].at[pl.ds(r, n)], sems.at[i, j]))
        for c in pair:
            c.start()
        copies.append(pair)
    warm = [stacked(wa[...]), stacked(wf[...])]
    pt[...] = jnp.zeros_like(pt)
    for (m, r, n, g, e, w, h, l), pair in zip(pieces, copies):
        for c in pair:
            c.wait()
        high, low = split(bufs[2 * m][pl.ds(r, n)] + bufs[2 * m + 1][pl.ds(r, n)])
        h[pl.ds(r, n)] = high
        l[pl.ds(r, n)] = low
        pt[:, pl.ds(plan.row_at[m] + r, n)] = three(warm[m], high, low, NT)


def load(plan, args, pieces):
    ag, ae, wa, fg, fe, wf = args
    bf = lambda m: jax.ShapeDtypeStruct((plan.rows[m], plan.cols[m]), jnp.bfloat16)
    f32 = lambda m: pltpu.VMEM((plan.rows[m], plan.cols[m]), jnp.float32)

    def body(*refs):
        load_kernel(plan, *refs[:11], refs[11:15], refs[15])

    return pl.pallas_call(
        body,
        out_shape=(bf(0), bf(0), bf(1), bf(1), jax.ShapeDtypeStruct((plan.rank, plan.row_all), jnp.float32)),
        in_specs=[ANY] * 4 + [VMEM] * 2,
        out_specs=(VMEM,) * 5,
        scratch_shapes=[f32(0), f32(0), f32(1), f32(1), pltpu.SemaphoreType.DMA((pieces, 2))],
        compiler_params=pltpu.CompilerParams(vmem_limit_bytes=36 * MIB),
        name="load",
    )(ag, ae, fg, fe, wa, wf)


def right_kernel(plan, count, scale, refs):
    place = lax.axis_index("shard")
    parts = refs[:count]
    rest = refs[count:]
    if scale is None:
        ha, la, hf, lf, slots, left, wide = rest
    else:
        inverse, ha, la, hf, lf, slots, left, wide = rest
    whole = tree([p[...] for p in parts])
    grams = []
    pairs = []
    for m in range(2):
        span = slice(plan.row_at[m], plan.row_at[m] + pad(plan.rows[m]))
        term = whole[:, span]
        if scale is not None:
            term = dot32(inverse[m], term, NN) * scale
        left[:, span] = term
        grams.append(dot32(term, term, NT))
        pairs.append(stacked(term[:, : plan.rows[m]]))
    gram = jnp.concatenate(grams + [jnp.zeros((plan.rank, LANES - 2 * plan.rank), jnp.float32)], axis=1)
    for m, (h, l) in enumerate(((ha, la), (hf, lf))):
        for c in range(0, plan.cols[m], 4 * LANES):
            n = min(4 * LANES, plan.cols[m] - c)
            wide[:, pl.ds(plan.col_at[m] + c, n)] = three(pairs[m], h[:, pl.ds(c, n)], l[:, pl.ds(c, n)], NN)
    used = plan.col_at[1] + pad(plan.cols[1])
    if used < plan.col_all:
        wide[:, used:] = jnp.zeros((plan.rank, plan.col_all - used), jnp.float32)
    for c in range(plan.shards):
        slot = slot_of(c, place, plan.shards)
        slots[slot, :, : plan.share] = wide[:, c * plan.share : (c + 1) * plan.share]
        slots[slot, :, plan.share :] = gram


def right(plan, parts, matrix, inverse=None, scale=None):
    f32 = jnp.float32
    extra = [] if scale is None else [inverse]
    return pl.pallas_call(
        lambda *refs: right_kernel(plan, len(parts), scale, refs),
        out_shape=(
            jax.ShapeDtypeStruct((plan.shards, plan.rank, plan.share + LANES), f32),
            jax.ShapeDtypeStruct((plan.rank, plan.row_all), f32),
        ),
        in_specs=[VMEM] * (len(parts) + len(extra) + 4),
        out_specs=(VMEM, VMEM),
        scratch_shapes=[pltpu.VMEM((plan.rank, plan.col_all), f32)],
        compiler_params=pltpu.CompilerParams(vmem_limit_bytes=8 * MIB),
        name="right",
    )(*parts, *extra, *matrix)


def gathered(plan, even, odd, wide):
    place = lax.axis_index("shard")
    for c in range(plan.shards):
        offset = lax.bitwise_xor(jnp.int32(c), place)
        row = offset >> 1
        wide[:, c * plan.share : (c + 1) * plan.share] = jnp.where((offset & 1) == 0, even[row], odd[row])


def left_kernel(plan, even, odd, ha, la, hf, lf, pt, wide):
    gathered(plan, even, odd, wide)
    pt[...] = jnp.zeros_like(pt)
    for m, (h, l) in enumerate(((ha, la), (hf, lf))):
        pair = stacked(wide[:, plan.col_at[m] : plan.col_at[m] + plan.cols[m]])
        for r in range(0, plan.rows[m], 2 * LANES):
            n = min(2 * LANES, plan.rows[m] - r)
            pt[:, pl.ds(plan.row_at[m] + r, n)] = three(pair, h[pl.ds(r, n)], l[pl.ds(r, n)], NT)


def left(plan, even, odd, matrix):
    return pl.pallas_call(
        functools.partial(left_kernel, plan),
        out_shape=jax.ShapeDtypeStruct((plan.rank, plan.row_all), jnp.float32),
        in_specs=[VMEM] * 6,
        out_specs=VMEM,
        scratch_shapes=[pltpu.VMEM((plan.rank, plan.col_all), jnp.float32)],
        compiler_params=pltpu.CompilerParams(vmem_limit_bytes=8 * MIB),
        name="left",
    )(even, odd, *matrix)


def factor_kernel(rank, scale, gram, out):
    row = lax.broadcasted_iota(jnp.int32, (rank, 2 * rank), 0)
    col = lax.broadcasted_iota(jnp.int32, (rank, 2 * rank), 1)
    eye = jnp.where(row + rank == col, 1.0, 0.0)
    below = lax.broadcasted_iota(jnp.int32, (rank, 1), 0)
    work = []
    for m in range(2):
        sym = gram[:, m * rank : (m + 1) * rank] * scale
        work.append(jnp.where(col < rank, jnp.concatenate([sym, sym], axis=1), eye))
    diag = [jnp.zeros((rank, 1), jnp.float32)] * 2
    for k in range(rank):
        for m in range(2):
            a = work[m]
            pivot = a[k : k + 1, k : k + 1]
            diag[m] = jnp.where(below == k, pivot, diag[m])
            ratio = jnp.where(below > k, a[:, k : k + 1], 0.0) / pivot
            work[m] = a - ratio * a[k : k + 1, :]
    for m in range(2):
        out[m] = work[m][:, rank:] / jnp.sqrt(diag[m])


def factor(plan, gram, scale):
    return pl.pallas_call(
        functools.partial(factor_kernel, plan.rank, scale),
        out_shape=jax.ShapeDtypeStruct((2, plan.rank, plan.rank), jnp.float32),
        in_specs=[VMEM],
        out_specs=VMEM,
        compiler_params=pltpu.CompilerParams(vmem_limit_bytes=2 * MIB),
        name="factor",
    )(gram)


def carry_kernel(plan, scale, even, odd, inverse, left, ha, la, hf, lf, ca, cf, qa, qf, wide, sa, sf, basis, sems):
    gathered(plan, even, odd, wide)
    triples = []
    for m, q in enumerate((qa, qf)):
        span = slice(plan.col_at[m], plan.col_at[m] + plan.cols[m])
        q[...] = dot32(inverse[m], wide[:, span], NN) * scale
        high, low = split(q[...])
        triples.append(jnp.concatenate([high, low, high], axis=0))
        term = dot32(inverse[m], left[:, plan.row_at[m] : plan.row_at[m] + pad(plan.rows[m])], NN)
        high, low = split(term)
        high, low = high.astype(jnp.float32), low.astype(jnp.float32)
        basis[pl.ds(plan.row_at[m], pad(plan.rows[m]))] = jnp.concatenate([high, high, low], axis=0).T.astype(jnp.bfloat16)
    copies = []
    for m, (h, l, s, out) in enumerate(((ha, la, sa, ca), (hf, lf, sf, cf))):
        for r in range(0, plan.rows[m], LANES):
            n = min(LANES, plan.rows[m] - r)
            b = basis[pl.ds(plan.row_at[m] + r, n)]
            s[pl.ds(r, n)] = h[pl.ds(r, n)].astype(jnp.float32) + l[pl.ds(r, n)].astype(jnp.float32) - dot(b, triples[m], NN)
            c = pltpu.make_async_copy(s.at[pl.ds(r, n)], out.at[0, pl.ds(r, n)], sems.at[len(copies)])
            c.start()
            copies.append(c)
    for c in copies:
        c.wait()


def carry(plan, even, odd, inverse, left, matrix, scale, pieces):
    f32 = jnp.float32
    rows, cols = plan.rows, plan.cols
    return pl.pallas_call(
        functools.partial(carry_kernel, plan, scale),
        out_shape=(
            jax.ShapeDtypeStruct((1, rows[0], cols[0]), f32),
            jax.ShapeDtypeStruct((1, rows[1], cols[1]), f32),
            jax.ShapeDtypeStruct((plan.rank, cols[0]), f32),
            jax.ShapeDtypeStruct((plan.rank, cols[1]), f32),
        ),
        in_specs=[VMEM] * 8,
        out_specs=(ANY, ANY, VMEM, VMEM),
        scratch_shapes=[
            pltpu.VMEM((plan.rank, plan.col_all), f32),
            pltpu.VMEM((rows[0], cols[0]), f32),
            pltpu.VMEM((rows[1], cols[1]), f32),
            pltpu.VMEM((plan.row_all, 3 * plan.rank), jnp.bfloat16),
            pltpu.SemaphoreType.DMA((pieces,)),
        ],
        compiler_params=pltpu.CompilerParams(vmem_limit_bytes=28 * MIB),
        name="carry",
    )(even, odd, inverse, left, *matrix)


def shuffle(x, axis, offset):
    size = lax.axis_size(axis)
    return lax.ppermute(x, axis, [(i, i ^ offset) for i in range(size)])


def exchanged(x, axis):
    return [x] + [shuffle(x, axis, k) for k in range(1, lax.axis_size(axis))]


def reduced(slots):
    half = slots.shape[0] // 2
    mine = slots[:half] + shuffle(slots[half:], "shard", 1)
    share = tree([mine[0]] + [shuffle(mine[j], "shard", 2 * j) for j in range(1, half)])
    return tree(exchanged(share, "dp"))


def spread(share, shards):
    even = jnp.stack([share] + [shuffle(share, "shard", 2 * j) for j in range(1, shards // 2)])
    return even, shuffle(even, "shard", 1)


def shards_fn(ag, ae, wa, fg, fe, wf):
    replicas = lax.axis_size("dp")
    plan = Plan((ag.shape[1], fg.shape[1]), (ag.shape[2], fg.shape[2]), wa.shape[0], lax.axis_size("shard"))
    pieces = sum(-(-r // LANES) for r in plan.rows)
    scale = 1.0 / replicas
    *matrix, terms = load(plan, (ag, ae, wa, fg, fe, wf), pieces)
    inverse = None
    for sweep in range(ITERS):
        parts = exchanged(terms, "dp")
        slots, whole = right(plan, parts, matrix, inverse, None if inverse is None else scale)
        share = reduced(slots)
        inverse = factor(plan, share[:, plan.share :], scale)
        even, odd = spread(share[:, : plan.share], plan.shards)
        if sweep + 1 < ITERS:
            terms = left(plan, even, odd, matrix)
    return carry(plan, even, odd, inverse, whole, matrix, scale, pieces)


def solution(mesh):
    tall = P("dp", "shard", None)
    return jax.shard_map(
        shards_fn,
        mesh=mesh,
        in_specs=(tall, tall, P(), tall, tall, P()),
        out_specs=(tall, tall, P(), P()),
        check_vma=False,
    )
```

```python
import functools

import jax
import jax.numpy as jnp
from jax import lax
from jax.experimental import pallas as pl
from jax.experimental.pallas import tpu as pltpu
from jax.sharding import PartitionSpec as P

ITERS = 2
LANES = 128
DEPTH = 3
MIB = 1 << 20

highest = lax.Precision.HIGHEST
NT = (((1,), (1,)), ((), ()))
NN = (((1,), (0,)), ((), ()))
VMEM = pl.BlockSpec(memory_space=pltpu.VMEM)
ANY = pl.BlockSpec(memory_space=pl.ANY)
HBM = pl.BlockSpec(memory_space=pltpu.HBM)


def dot(a, b, dims):
    return lax.dot_general(a, b, dims, preferred_element_type=jnp.float32)


def dot32(a, b, dims):
    return lax.dot_general(a, b, dims, precision=highest, preferred_element_type=jnp.float32)


def pad(n):
    return -(-n // LANES) * LANES


def split(x):
    high = x.astype(jnp.bfloat16)
    low = (x - high.astype(jnp.float32)).astype(jnp.bfloat16)
    return high, low


def stacked(x):
    high, low = split(x)
    return jnp.concatenate([high, low], axis=0)


def tree(terms):
    terms = list(terms)
    while len(terms) > 1:
        half = len(terms) // 2
        terms = [terms[k] + terms[k + half] for k in range(half)]
    return terms[0]


def three(pair, high, low, dims):
    rank = pair.shape[0] // 2
    first = dot(pair, high, dims)
    return first[:rank] + first[rank:] + dot(pair[:rank], low, dims)


class Plan:
    def __init__(self, rows, cols, rank, shards):
        self.rows, self.cols, self.rank, self.shards = rows, cols, rank, shards
        self.half = shards // 2
        self.row_at = (0, pad(rows[0]))
        self.row_all = pad(rows[0]) + pad(rows[1])
        self.part = tuple(pad(-(-c // shards)) for c in cols)
        self.part_at = (0, self.part[0])
        self.share = sum(self.part)
        self.padded = tuple(p * shards for p in self.part)

    def row_span(self, m):
        return slice(self.row_at[m], self.row_at[m] + pad(self.rows[m]))

    def part_span(self, m):
        return slice(self.part_at[m], self.part_at[m] + self.part[m])

    def columns(self, m, chunk):
        return pl.ds(pl.multiple_of(chunk * self.part[m], LANES), self.part[m])


def params(limit):
    return pltpu.CompilerParams(vmem_limit_bytes=int(limit * MIB))


def cost(us):
    return pl.CostEstimate(flops=0, transcendentals=0, bytes_accessed=int(us * 3.0e6))


def chunk_of(slot):
    return lax.bitwise_xor(jnp.int32(slot), lax.axis_index("shard"))


def blank(plan, m, high, low, out):
    if pad(plan.rows[m]) > plan.rows[m]:
        out[...] = jnp.zeros_like(out)
    if plan.padded[m] > plan.cols[m]:
        none = jnp.zeros((plan.rows[m], plan.padded[m] - plan.cols[m]), jnp.bfloat16)
        high[:, plan.cols[m] :] = none
        low[:, plan.cols[m] :] = none


def load_rows(plan, m, rows, pair, grad, error, high, low, out):
    h, l = split(grad + error)
    high[rows, : plan.cols[m]] = h
    low[rows, : plan.cols[m]] = l
    out[:, rows] = three(pair, h, l, NT)


def blocks(count):
    return [pl.ds(r, min(LANES, count - r)) for r in range(0, count, LANES)]


def stream_kernel(plan, m, grad, error, warm, high, low, out, gbuf, ebuf, wbuf, sems, wsem):
    first = pltpu.make_async_copy(warm, wbuf, wsem.at[0])
    first.start()
    pieces = []
    for rows in blocks(plan.rows[m]):
        both = ((grad, gbuf), (error, ebuf))
        pieces.append((rows, [pltpu.make_async_copy(src.at[0, rows], buf.at[rows], sems.at[len(pieces), j]) for j, (src, buf) in enumerate(both)]))

    def start(i):
        for c in pieces[i][1] if i < len(pieces) else ():
            c.start()

    for i in range(DEPTH):
        start(i)
    blank(plan, m, high, low, out)
    first.wait()
    pair = stacked(wbuf[...])
    for i, (rows, copies) in enumerate(pieces):
        for c in copies:
            c.wait()
        start(i + DEPTH)
        load_rows(plan, m, rows, pair, gbuf[rows], ebuf[rows], high, low, out)


def hold_kernel(plan, m, grad, error, warm, high, low, out):
    blank(plan, m, high, low, out)
    pair = stacked(warm[...])
    for rows in blocks(plan.rows[m]):
        load_rows(plan, m, rows, pair, grad[0, rows], error[0, rows], high, low, out)


def load(plan, m, args, stream):
    half = jax.ShapeDtypeStruct((plan.rows[m], plan.padded[m]), jnp.bfloat16)
    full = pltpu.VMEM((plan.rows[m], plan.cols[m]), jnp.float32)
    outs = (half, half, f32(plan.rank, pad(plan.rows[m])))
    if not stream:
        return pl.pallas_call(
            functools.partial(hold_kernel, plan, m),
            out_shape=outs,
            in_specs=[VMEM] * 3,
            out_specs=(VMEM,) * 3,
            compiler_params=params(6),
            cost_estimate=cost(4),
            name="hold",
        )(*args)
    scratch = [full, full, pltpu.VMEM((plan.rank, plan.cols[m]), jnp.float32)]
    sems = [pltpu.SemaphoreType.DMA((len(blocks(plan.rows[m])), 2)), pltpu.SemaphoreType.DMA((1,))]
    return pl.pallas_call(
        functools.partial(stream_kernel, plan, m),
        out_shape=outs,
        in_specs=[ANY] * 3,
        out_specs=(VMEM,) * 3,
        scratch_shapes=scratch + sems,
        compiler_params=params(18),
        cost_estimate=cost(7),
        name="stream",
    )(*[pltpu.with_memory_space_constraint(a, pltpu.HBM) for a in args])


def right_slots(plan, m, odd, left, high, low, slots):
    pair = stacked(left[:, : plan.rows[m]])
    for j in range(plan.half):
        at = plan.columns(m, chunk_of(2 * j + odd))
        slots[j, :, plan.part_span(m)] = three(pair, high[:, at], low[:, at], NN)


def right_begin(m, scale, parts, inverse, left):
    term = parts[0][...] + parts[1][...]
    if scale is not None:
        term = dot32(inverse[m], term, NN) * scale
    left[...] = term
    return dot32(term, term, NT)


def gram_span(plan, m):
    return slice(plan.share + m * plan.rank, plan.share + (m + 1) * plan.rank)


def right_first_kernel(plan, m, scale, *refs):
    *inputs, odd, even, left = refs
    *parts_inverse, high, low = inputs
    gram = right_begin(m, scale, parts_inverse[:2], parts_inverse[-1], left)
    for parity, slots in enumerate((even, odd)):
        slots[:, :, plan.share :] = jnp.zeros((plan.half, plan.rank, LANES), jnp.float32)
        for j in range(plan.half):
            slots[j, :, gram_span(plan, m)] = gram
        right_slots(plan, m, parity, left, high, low, slots)


def right_odd_kernel(plan, m, scale, *refs):
    *inputs, odd, left, gram = refs
    *parts_inverse, _, high, low = inputs
    gram[...] = right_begin(m, scale, parts_inverse[:2], parts_inverse[-1], left)
    for j in range(plan.half):
        odd[j, :, gram_span(plan, m)] = gram[...]
    right_slots(plan, m, 1, left, high, low, odd)


def right_even_kernel(plan, m, left, gram, _, high, low, even):
    for j in range(plan.half):
        even[j, :, gram_span(plan, m)] = gram[...]
    right_slots(plan, m, 0, left, high, low, even)


def f32(*shape):
    return jax.ShapeDtypeStruct(shape, jnp.float32)


def right(plan, parts, matrix, inverse=None, scale=None):
    extra = [] if scale is None else [inverse]
    slots = f32(plan.half, plan.rank, plan.share + LANES)
    lefts = [f32(plan.rank, pad(r)) for r in plan.rows]

    def call(kernel, operands, outs, us, aliases={}):
        return pl.pallas_call(
            kernel,
            out_shape=outs,
            in_specs=[VMEM] * len(operands),
            out_specs=(VMEM,) * len(outs),
            input_output_aliases=aliases,
            compiler_params=params(5),
            cost_estimate=cost(us),
        )(*operands)

    first = functools.partial(right_first_kernel, plan, 1, scale)
    odd, even, left_1 = call(first, [*parts[1], *extra, *matrix[2:]], (slots, slots, lefts[1]), 1.8)
    second = functools.partial(right_odd_kernel, plan, 0, scale)
    operands = [*parts[0], *extra, odd, *matrix[:2]]
    odd, left_0, gram = call(second, operands, (slots, lefts[0], f32(plan.rank, plan.rank)), 1, {len(operands) - 3: 0})
    third = functools.partial(right_even_kernel, plan, 0)
    (even,) = call(third, [left_0, gram, even, *matrix[:2]], (slots,), 1, {2: 0})
    return odd, even, (left_0, left_1)


def left_kernel(plan, m, odd, *refs):
    *inputs, high, low, out = refs
    slots = inputs[0]
    if not odd and pad(plan.rows[m]) > plan.rows[m]:
        out[...] = jnp.zeros_like(out)
    if odd and pad(plan.rows[m]) > plan.rows[m]:
        out[:, plan.rows[m] :] = jnp.zeros((plan.rank, pad(plan.rows[m]) - plan.rows[m]), jnp.float32)
    terms = [(stacked(slots[j, :, plan.part_span(m)]), plan.columns(m, chunk_of(2 * j + odd))) for j in range(plan.half)]
    for r in range(0, plan.rows[m], 2 * LANES):
        rows = pl.ds(r, min(2 * LANES, plan.rows[m] - r))
        total = inputs[1][:, rows] if odd else None
        for pair, cols in terms:
            term = three(pair, high[rows, cols], low[rows, cols], NT)
            total = term if total is None else total + term
        out[:, rows] = total


def left(plan, near, far, matrix):
    def call(m, parity, *operands):
        return pl.pallas_call(
            functools.partial(left_kernel, plan, m, parity),
            out_shape=f32(plan.rank, pad(plan.rows[m])),
            in_specs=[VMEM] * (len(operands) + 2),
            out_specs=VMEM,
            compiler_params=params(5),
            cost_estimate=cost(1.2),
        )(*operands, *matrix[2 * m : 2 * m + 2])

    return [call(m, 1, far, call(m, 0, near)) for m in range(2)]


def factor_kernel(rank, gram, out):
    row = lax.broadcasted_iota(jnp.int32, (rank, 2 * rank), 0)
    col = lax.broadcasted_iota(jnp.int32, (rank, 2 * rank), 1)
    eye = jnp.where(row + rank == col, 1.0, 0.0)
    below = lax.broadcasted_iota(jnp.int32, (rank, 1), 0)
    work = []
    for m in range(2):
        sym = gram[:, m * rank : (m + 1) * rank]
        work.append(jnp.where(col < rank, jnp.concatenate([sym, sym], axis=1), eye))
    diag = [jnp.zeros((rank, 1), jnp.float32)] * 2
    for k in range(rank):
        for m in range(2):
            a = work[m]
            pivot = a[k : k + 1, k : k + 1]
            diag[m] = jnp.where(below == k, pivot, diag[m])
            ratio = jnp.where(below > k, a[:, k : k + 1], 0.0) / pivot
            work[m] = a - ratio * a[k : k + 1, :]
    for m in range(2):
        out[m] = work[m][:, rank:] / jnp.sqrt(diag[m])


def factor(plan, gram):
    return pl.pallas_call(
        functools.partial(factor_kernel, plan.rank),
        out_shape=jax.ShapeDtypeStruct((2, plan.rank, plan.rank), jnp.float32),
        in_specs=[VMEM],
        out_specs=VMEM,
        compiler_params=params(2),
        cost_estimate=cost(3),
        name="factor",
    )(gram)


def carry_slots(plan, scale, odd, slots, inverse, basis, matrix, q, stages, outs, sems):
    jobs = []
    for j in range(plan.half):
        chunk = chunk_of(2 * j + odd)
        for m, (h, l) in enumerate((matrix[:2], matrix[2:])):
            span = plan.part_span(m)
            q[j, :, span] = dot32(inverse[m], slots[j, :, span], NN) * scale
            high, low = split(q[j, :, span])
            triple = jnp.concatenate([high, low, high], axis=0)
            at = plan.columns(m, chunk)
            for r in range(0, plan.rows[m], 2 * LANES):
                rows = pl.ds(r, min(2 * LANES, plan.rows[m] - r))
                b = basis[pl.ds(plan.row_at[m] + r, rows.size)]
                whole = h[rows, at].astype(jnp.float32) + l[rows, at].astype(jnp.float32)
                stages[m][j, rows] = whole - dot(b, triple, NN)
            last = plan.cols[m] - (plan.shards - 1) * plan.part[m]

            def copy(m=m, j=j, at=at, n=plan.part[m]):
                at = at if n == plan.part[m] else pl.ds(plan.cols[m] - n, n)
                return pltpu.make_async_copy(stages[m].at[j, :, pl.ds(0, n)], outs[m].at[0, :, at], sems.at[m, j])

            def each(act, copy=copy, chunk=chunk, last=last, full=last == plan.part[m]):
                if full:
                    act(copy())
                else:
                    pl.when(chunk < plan.shards - 1)(lambda: act(copy()))
                    pl.when(chunk == plan.shards - 1)(lambda: act(copy(n=last)))

            each(lambda c: c.start())
            jobs.append(each)
    for each in jobs:
        each(lambda c: c.wait())


def basis_kernel(plan, inverse, left_0, left_1, basis):
    for m in range(2):
        high, low = split(dot32(inverse[m], (left_0, left_1)[m][...], NN))
        high, low = high.astype(jnp.float32), low.astype(jnp.float32)
        basis[plan.row_span(m)] = jnp.concatenate([high, high, low], axis=0).T.astype(jnp.bfloat16)


def basis_of(plan, inverse, left):
    return pl.pallas_call(
        functools.partial(basis_kernel, plan),
        out_shape=jax.ShapeDtypeStruct((plan.row_all, 3 * plan.rank), jnp.bfloat16),
        in_specs=[VMEM] * 3,
        out_specs=VMEM,
        compiler_params=params(4),
        cost_estimate=cost(0.8),
        name="basis",
    )(inverse, *left)


def carry_first_kernel(plan, scale, slots, inverse, basis, ha, la, hf, lf, ca, cf, q, sa, sf, sems):
    carry_slots(plan, scale, 0, slots, inverse, basis, (ha, la, hf, lf), q, (sa, sf), (ca, cf), sems)


def carry_second_kernel(plan, scale, slots, inverse, basis, other, ia, jf, ha, la, hf, lf, ca, cf, qa, qf, q, sa, sf, sems):
    carry_slots(plan, scale, 1, slots, inverse, basis, (ha, la, hf, lf), q, (sa, sf), (ca, cf), sems)
    place = lax.axis_index("shard")
    for c in range(plan.shards):
        slot = lax.bitwise_xor(jnp.int32(c), place)
        row = slot >> 1
        for m, out in enumerate((qa, qf)):
            start = c * plan.part[m]
            n = min(plan.part[m], plan.cols[m] - start)
            span = slice(plan.part_at[m], plan.part_at[m] + n)
            out[:, start : start + n] = jnp.where((slot & 1) == 0, other[row, :, span], q[row, :, span])


def carry(plan, even, odd, inverse, basis, matrix, scale):
    half, rank, rows, cols = plan.half, plan.rank, plan.rows, plan.cols
    stage = [pltpu.VMEM((half, rows[m], plan.part[m]), jnp.float32) for m in range(2)] + [pltpu.SemaphoreType.DMA((2, half))]
    outs = tuple(f32(1, rows[m], cols[m]) for m in range(2))
    ca, cf, q = pl.pallas_call(
        functools.partial(carry_first_kernel, plan, scale),
        out_shape=outs + (f32(half, rank, plan.share),),
        in_specs=[VMEM] * 7,
        out_specs=(ANY, ANY, VMEM),
        scratch_shapes=stage,
        compiler_params=params(16),
        cost_estimate=cost(4),
        name="carry_first",
    )(even, inverse, basis, *matrix)
    return pl.pallas_call(
        functools.partial(carry_second_kernel, plan, scale),
        out_shape=outs + tuple(f32(rank, cols[m]) for m in range(2)),
        in_specs=[VMEM] * 4 + [ANY] * 2 + [VMEM] * 4,
        out_specs=(ANY, ANY, VMEM, VMEM),
        scratch_shapes=[pltpu.VMEM((half, rank, plan.share), jnp.float32)] + stage,
        input_output_aliases={4: 0, 5: 1},
        compiler_params=params(16),
        cost_estimate=cost(4),
        name="carry_second",
    )(odd, inverse, basis, q, ca, cf, *matrix)


def swapped(x, axis, offset):
    return lax.ppermute(x, axis, [(i, i ^ offset) for i in range(lax.axis_size(axis))])


def exchanged(x, axis):
    return [x] + [swapped(x, axis, k) for k in range(1, lax.axis_size(axis))]


def offsets(size):
    found = [size - 1]
    while found[-1] > 1:
        found.append(found[-1] // 2)
    return found


def paired(terms, axis):
    hops = offsets(lax.axis_size(axis))
    parts = []
    for m, x in enumerate(terms):
        order = hops if m else hops[::-1]
        for step, offset in enumerate(order):
            y = swapped(x, axis, offset)
            if step + 1 < len(order):
                x = x + y
        parts.append((x, y))
    return parts


def gathered(odd, even):
    mine = even + swapped(odd, "shard", 1)
    return tree([mine[0]] + [swapped(mine[j], "shard", 2 * j) for j in range(1, mine.shape[0])])


def spread(share, half):
    return jnp.stack([share] + [swapped(share, "shard", 2 * j) for j in range(1, half)])


def compress(ag, ae, wa, fg, fe, wf):
    plan = Plan((ag.shape[1], fg.shape[1]), (ag.shape[2], fg.shape[2]), wa.shape[0], lax.axis_size("shard"))
    scale = 1.0 / lax.axis_size("dp")
    *second, left_1 = load(plan, 1, (fg, fe, wf), True)
    *first, left_0 = load(plan, 0, (ag, ae, wa), False)
    matrix = first + second
    terms = [left_0, left_1]
    inverse = None
    for sweep in range(ITERS):
        parts = paired(terms, "dp")
        odd, even, whole = right(plan, parts, matrix, inverse, None if inverse is None else scale)
        joint = gathered(odd, even)
        inverse = factor(plan, joint[:, plan.share :])
        share = tree(exchanged(joint[:, : plan.share], "dp"))
        if sweep + 1 == ITERS:
            basis = basis_of(plan, inverse, whole)
            share, inverse, basis = lax.optimization_barrier((share, inverse, basis))
        else:
            share, inverse = lax.optimization_barrier((share, inverse))
        near = spread(share, plan.half)
        far = swapped(near, "shard", 1)
        if sweep + 1 < ITERS:
            terms = left(plan, near, far, matrix)
    return carry(plan, near, far, inverse, basis, matrix, scale)


def solution(mesh):
    tall = P("dp", "shard", None)
    return jax.shard_map(
        compress,
        mesh=mesh,
        in_specs=(tall, tall, P(), tall, tall, P()),
        out_specs=(tall, tall, P(), P()),
        check_vma=False,
    )
```

```python
import functools

import jax
import jax.numpy as jnp
from jax import lax
from jax.experimental import pallas as pl
from jax.experimental.pallas import tpu as pltpu
from jax.sharding import PartitionSpec as P

ITERS = 2
LANES = 128
DEPTH = 3
MIB = 1 << 20

highest = lax.Precision.HIGHEST
NT = (((1,), (1,)), ((), ()))
NN = (((1,), (0,)), ((), ()))
VMEM = pl.BlockSpec(memory_space=pltpu.VMEM)
ANY = pl.BlockSpec(memory_space=pl.ANY)
HBM = pl.BlockSpec(memory_space=pltpu.HBM)


def dot(a, b, dims):
    return lax.dot_general(a, b, dims, preferred_element_type=jnp.float32)


def dot32(a, b, dims):
    return lax.dot_general(a, b, dims, precision=highest, preferred_element_type=jnp.float32)


def pad(n):
    return -(-n // LANES) * LANES


def split(x):
    high = x.astype(jnp.bfloat16)
    low = (x - high.astype(jnp.float32)).astype(jnp.bfloat16)
    return high, low


def stacked(x):
    high, low = split(x)
    return jnp.concatenate([high, low], axis=0)


def tree(terms):
    terms = list(terms)
    while len(terms) > 1:
        half = len(terms) // 2
        terms = [terms[k] + terms[k + half] for k in range(half)]
    return terms[0]


def three(pair, high, low, dims):
    rank = pair.shape[0] // 2
    first = dot(pair, high, dims)
    return first[:rank] + first[rank:] + dot(pair[:rank], low, dims)


class Plan:
    def __init__(self, rows, cols, rank, shards):
        self.rows, self.cols, self.rank, self.shards = rows, cols, rank, shards
        self.half = shards // 2
        self.row_at = (0, pad(rows[0]))
        self.row_all = pad(rows[0]) + pad(rows[1])
        self.part = tuple(pad(-(-c // shards)) for c in cols)
        self.part_at = (0, self.part[0])
        self.share = sum(self.part)
        self.padded = tuple(p * shards for p in self.part)

    def row_span(self, m):
        return slice(self.row_at[m], self.row_at[m] + pad(self.rows[m]))

    def part_span(self, m):
        return slice(self.part_at[m], self.part_at[m] + self.part[m])

    def columns(self, m, chunk):
        return pl.ds(pl.multiple_of(chunk * self.part[m], LANES), self.part[m])


def params(limit):
    return pltpu.CompilerParams(vmem_limit_bytes=int(limit * MIB))


def cost(us):
    return pl.CostEstimate(flops=0, transcendentals=0, bytes_accessed=int(us * 3.0e6))


def chunk_of(slot):
    return lax.bitwise_xor(jnp.int32(slot), lax.axis_index("shard"))


def blank(plan, m, high, low, out):
    if pad(plan.rows[m]) > plan.rows[m]:
        out[...] = jnp.zeros_like(out)
    if plan.padded[m] > plan.cols[m]:
        none = jnp.zeros((plan.rows[m], plan.padded[m] - plan.cols[m]), jnp.bfloat16)
        high[:, plan.cols[m] :] = none
        low[:, plan.cols[m] :] = none


def load_rows(plan, m, rows, pair, grad, error, high, low, out):
    h, l = split(grad + error)
    high[rows, : plan.cols[m]] = h
    low[rows, : plan.cols[m]] = l
    out[:, rows] = three(pair, h, l, NT)


def blocks(count):
    return [pl.ds(r, min(LANES, count - r)) for r in range(0, count, LANES)]


def stream_kernel(plan, m, grad, error, warm, high, low, out, gbuf, ebuf, wbuf, sems, wsem):
    first = pltpu.make_async_copy(warm, wbuf, wsem.at[0])
    first.start()
    pieces = []
    for rows in blocks(plan.rows[m]):
        both = ((grad, gbuf), (error, ebuf))
        pieces.append((rows, [pltpu.make_async_copy(src.at[0, rows], buf.at[rows], sems.at[len(pieces), j]) for j, (src, buf) in enumerate(both)]))

    def start(i):
        for c in pieces[i][1] if i < len(pieces) else ():
            c.start()

    for i in range(DEPTH):
        start(i)
    blank(plan, m, high, low, out)
    first.wait()
    pair = stacked(wbuf[...])
    for i, (rows, copies) in enumerate(pieces):
        for c in copies:
            c.wait()
        start(i + DEPTH)
        load_rows(plan, m, rows, pair, gbuf[rows], ebuf[rows], high, low, out)


def hold_kernel(plan, m, grad, error, warm, high, low, out):
    blank(plan, m, high, low, out)
    pair = stacked(warm[...])
    for rows in blocks(plan.rows[m]):
        load_rows(plan, m, rows, pair, grad[0, rows], error[0, rows], high, low, out)


def load(plan, m, args, stream):
    half = jax.ShapeDtypeStruct((plan.rows[m], plan.padded[m]), jnp.bfloat16)
    full = pltpu.VMEM((plan.rows[m], plan.cols[m]), jnp.float32)
    outs = (half, half, f32(plan.rank, pad(plan.rows[m])))
    if not stream:
        return pl.pallas_call(
            functools.partial(hold_kernel, plan, m),
            out_shape=outs,
            in_specs=[VMEM] * 3,
            out_specs=(VMEM,) * 3,
            compiler_params=params(6),
            cost_estimate=cost(4),
            name="hold",
        )(*args)
    scratch = [full, full, pltpu.VMEM((plan.rank, plan.cols[m]), jnp.float32)]
    sems = [pltpu.SemaphoreType.DMA((len(blocks(plan.rows[m])), 2)), pltpu.SemaphoreType.DMA((1,))]
    return pl.pallas_call(
        functools.partial(stream_kernel, plan, m),
        out_shape=outs,
        in_specs=[ANY] * 3,
        out_specs=(VMEM,) * 3,
        scratch_shapes=scratch + sems,
        compiler_params=params(18),
        cost_estimate=cost(7),
        name="stream",
    )(*[pltpu.with_memory_space_constraint(a, pltpu.HBM) for a in args])


def right_slots(plan, m, odd, left, high, low, slots):
    pair = stacked(left[:, : plan.rows[m]])
    for j in range(plan.half):
        at = plan.columns(m, chunk_of(2 * j + odd))
        slots[j, :, plan.part_span(m)] = three(pair, high[:, at], low[:, at], NN)


def right_begin(m, scale, parts, inverse, left):
    term = parts[0][...] + parts[1][...]
    if scale is not None:
        term = dot32(inverse[m], term, NN) * scale
    left[...] = term
    return dot32(term, term, NT)


def gram_span(plan, m):
    return slice(plan.share + m * plan.rank, plan.share + (m + 1) * plan.rank)


def right_first_kernel(plan, m, scale, *refs):
    *inputs, odd, even, left = refs
    *parts_inverse, high, low = inputs
    gram = right_begin(m, scale, parts_inverse[:2], parts_inverse[-1], left)
    for parity, slots in enumerate((even, odd)):
        slots[:, :, plan.share :] = jnp.zeros((plan.half, plan.rank, LANES), jnp.float32)
        for j in range(plan.half):
            slots[j, :, gram_span(plan, m)] = gram
        right_slots(plan, m, parity, left, high, low, slots)


def right_odd_kernel(plan, m, scale, *refs):
    *inputs, odd, left, gram = refs
    *parts_inverse, _, high, low = inputs
    gram[...] = right_begin(m, scale, parts_inverse[:2], parts_inverse[-1], left)
    for j in range(plan.half):
        odd[j, :, gram_span(plan, m)] = gram[...]
    right_slots(plan, m, 1, left, high, low, odd)


def right_even_kernel(plan, m, left, gram, _, high, low, even):
    for j in range(plan.half):
        even[j, :, gram_span(plan, m)] = gram[...]
    right_slots(plan, m, 0, left, high, low, even)


def f32(*shape):
    return jax.ShapeDtypeStruct(shape, jnp.float32)


def right(plan, parts, matrix, inverse=None, scale=None):
    extra = [] if scale is None else [inverse]
    slots = f32(plan.half, plan.rank, plan.share + LANES)
    lefts = [f32(plan.rank, pad(r)) for r in plan.rows]

    def call(kernel, operands, outs, us, aliases={}):
        return pl.pallas_call(
            kernel,
            out_shape=outs,
            in_specs=[VMEM] * len(operands),
            out_specs=(VMEM,) * len(outs),
            input_output_aliases=aliases,
            compiler_params=params(5),
            cost_estimate=cost(us),
        )(*operands)

    first = functools.partial(right_first_kernel, plan, 1, scale)
    odd, even, left_1 = call(first, [*parts[1], *extra, *matrix[2:]], (slots, slots, lefts[1]), 1.8)
    second = functools.partial(right_odd_kernel, plan, 0, scale)
    operands = [*parts[0], *extra, odd, *matrix[:2]]
    odd, left_0, gram = call(second, operands, (slots, lefts[0], f32(plan.rank, plan.rank)), 1, {len(operands) - 3: 0})
    third = functools.partial(right_even_kernel, plan, 0)
    (even,) = call(third, [left_0, gram, even, *matrix[:2]], (slots,), 1, {2: 0})
    return odd, even, (left_0, left_1)


def left_kernel(plan, m, odd, *refs):
    *inputs, high, low, out = refs
    slots = inputs[0]
    if not odd and pad(plan.rows[m]) > plan.rows[m]:
        out[...] = jnp.zeros_like(out)
    if odd and pad(plan.rows[m]) > plan.rows[m]:
        out[:, plan.rows[m] :] = jnp.zeros((plan.rank, pad(plan.rows[m]) - plan.rows[m]), jnp.float32)
    terms = [(stacked(slots[j, :, plan.part_span(m)]), plan.columns(m, chunk_of(2 * j + odd))) for j in range(plan.half)]
    for r in range(0, plan.rows[m], 2 * LANES):
        rows = pl.ds(r, min(2 * LANES, plan.rows[m] - r))
        total = inputs[1][:, rows] if odd else None
        for pair, cols in terms:
            term = three(pair, high[rows, cols], low[rows, cols], NT)
            total = term if total is None else total + term
        out[:, rows] = total


def left(plan, near, far, matrix):
    def call(m, parity, *operands):
        return pl.pallas_call(
            functools.partial(left_kernel, plan, m, parity),
            out_shape=f32(plan.rank, pad(plan.rows[m])),
            in_specs=[VMEM] * (len(operands) + 2),
            out_specs=VMEM,
            compiler_params=params(5),
            cost_estimate=cost(1.2),
        )(*operands, *matrix[2 * m : 2 * m + 2])

    return [call(m, 1, far, call(m, 0, near)) for m in range(2)]


def factor_kernel(rank, gram, out):
    row = lax.broadcasted_iota(jnp.int32, (rank, 2 * rank), 0)
    col = lax.broadcasted_iota(jnp.int32, (rank, 2 * rank), 1)
    eye = jnp.where(row + rank == col, 1.0, 0.0)
    below = lax.broadcasted_iota(jnp.int32, (rank, 1), 0)
    work = []
    for m in range(2):
        sym = gram[:, m * rank : (m + 1) * rank]
        work.append(jnp.where(col < rank, jnp.concatenate([sym, sym], axis=1), eye))
    diag = [jnp.zeros((rank, 1), jnp.float32)] * 2
    for k in range(rank):
        for m in range(2):
            a = work[m]
            pivot = a[k : k + 1, k : k + 1]
            diag[m] = jnp.where(below == k, pivot, diag[m])
            ratio = jnp.where(below > k, a[:, k : k + 1], 0.0) / pivot
            work[m] = a - ratio * a[k : k + 1, :]
    for m in range(2):
        out[m] = work[m][:, rank:] / jnp.sqrt(diag[m])


def factor(plan, gram):
    return pl.pallas_call(
        functools.partial(factor_kernel, plan.rank),
        out_shape=jax.ShapeDtypeStruct((2, plan.rank, plan.rank), jnp.float32),
        in_specs=[VMEM],
        out_specs=VMEM,
        compiler_params=params(2),
        cost_estimate=cost(3),
        name="factor",
    )(gram)


def carry_slots(plan, scale, odd, slots, inverse, basis, matrix, q, stages, outs, sems):
    jobs = []
    triples = []
    for m in range(2):
        term = jnp.concatenate([slots[j, :, plan.part_span(m)] for j in range(plan.half)], axis=1)
        term = dot32(inverse[m], term, NN) * scale
        high, low = split(term)
        triples.append(jnp.concatenate([high, low, high], axis=0))
        for j in range(plan.half):
            q[j, :, plan.part_span(m)] = term[:, j * plan.part[m] : (j + 1) * plan.part[m]]
    for j in range(plan.half):
        chunk = chunk_of(2 * j + odd)
        for m, (h, l) in enumerate((matrix[:2], matrix[2:])):
            triple = triples[m][:, j * plan.part[m] : (j + 1) * plan.part[m]]
            at = plan.columns(m, chunk)
            for r in range(0, plan.rows[m], 2 * LANES):
                rows = pl.ds(r, min(2 * LANES, plan.rows[m] - r))
                b = basis[pl.ds(plan.row_at[m] + r, rows.size)]
                whole = h[rows, at].astype(jnp.float32) + l[rows, at].astype(jnp.float32)
                stages[m][j, rows] = whole - dot(b, triple, NN)
            last = plan.cols[m] - (plan.shards - 1) * plan.part[m]

            def copy(m=m, j=j, at=at, n=plan.part[m]):
                at = at if n == plan.part[m] else pl.ds(plan.cols[m] - n, n)
                return pltpu.make_async_copy(stages[m].at[j, :, pl.ds(0, n)], outs[m].at[0, :, at], sems.at[m, j])

            def each(act, copy=copy, chunk=chunk, last=last, full=last == plan.part[m]):
                if full:
                    act(copy())
                else:
                    pl.when(chunk < plan.shards - 1)(lambda: act(copy()))
                    pl.when(chunk == plan.shards - 1)(lambda: act(copy(n=last)))

            each(lambda c: c.start())
            jobs.append(each)
    for each in jobs:
        each(lambda c: c.wait())


def basis_kernel(plan, inverse, left_0, left_1, basis):
    for m in range(2):
        high, low = split(dot32(inverse[m], (left_0, left_1)[m][...], NN))
        high, low = high.astype(jnp.float32), low.astype(jnp.float32)
        basis[plan.row_span(m)] = jnp.concatenate([high, high, low], axis=0).T.astype(jnp.bfloat16)


def basis_of(plan, inverse, left):
    return pl.pallas_call(
        functools.partial(basis_kernel, plan),
        out_shape=jax.ShapeDtypeStruct((plan.row_all, 3 * plan.rank), jnp.bfloat16),
        in_specs=[VMEM] * 3,
        out_specs=VMEM,
        compiler_params=params(4),
        cost_estimate=cost(0.8),
        name="basis",
    )(inverse, *left)


def carry_first_kernel(plan, scale, slots, inverse, basis, ha, la, hf, lf, ca, cf, q, sa, sf, sems):
    carry_slots(plan, scale, 0, slots, inverse, basis, (ha, la, hf, lf), q, (sa, sf), (ca, cf), sems)


def carry_second_kernel(plan, scale, slots, inverse, basis, other, ia, jf, ha, la, hf, lf, ca, cf, qa, qf, q, sa, sf, sems):
    carry_slots(plan, scale, 1, slots, inverse, basis, (ha, la, hf, lf), q, (sa, sf), (ca, cf), sems)
    place = lax.axis_index("shard")
    for c in range(plan.shards):
        slot = lax.bitwise_xor(jnp.int32(c), place)
        row = slot >> 1
        for m, out in enumerate((qa, qf)):
            start = c * plan.part[m]
            n = min(plan.part[m], plan.cols[m] - start)
            span = slice(plan.part_at[m], plan.part_at[m] + n)
            out[:, start : start + n] = jnp.where((slot & 1) == 0, other[row, :, span], q[row, :, span])


def carry(plan, even, odd, inverse, basis, matrix, scale):
    half, rank, rows, cols = plan.half, plan.rank, plan.rows, plan.cols
    stage = [pltpu.VMEM((half, rows[m], plan.part[m]), jnp.float32) for m in range(2)] + [pltpu.SemaphoreType.DMA((2, half))]
    outs = tuple(f32(1, rows[m], cols[m]) for m in range(2))
    ca, cf, q = pl.pallas_call(
        functools.partial(carry_first_kernel, plan, scale),
        out_shape=outs + (f32(half, rank, plan.share),),
        in_specs=[VMEM] * 7,
        out_specs=(ANY, ANY, VMEM),
        scratch_shapes=stage,
        compiler_params=params(16),
        cost_estimate=cost(4),
        name="carry_first",
    )(even, inverse, basis, *matrix)
    return pl.pallas_call(
        functools.partial(carry_second_kernel, plan, scale),
        out_shape=outs + tuple(f32(rank, cols[m]) for m in range(2)),
        in_specs=[VMEM] * 4 + [ANY] * 2 + [VMEM] * 4,
        out_specs=(ANY, ANY, VMEM, VMEM),
        scratch_shapes=[pltpu.VMEM((half, rank, plan.share), jnp.float32)] + stage,
        input_output_aliases={4: 0, 5: 1},
        compiler_params=params(16),
        cost_estimate=cost(4),
        name="carry_second",
    )(odd, inverse, basis, q, ca, cf, *matrix)


def swapped(x, axis, offset):
    return lax.ppermute(x, axis, [(i, i ^ offset) for i in range(lax.axis_size(axis))])


def turned(x, axis, offset):
    size = lax.axis_size(axis)
    return lax.ppermute(x, axis, [(i, (i + offset) % size) for i in range(size)])


def exchanged(x, axis):
    size = lax.axis_size(axis)
    terms = [x]
    for k in range(1, size):
        terms.append(turned(x, axis, k))
    return terms


def offsets(size):
    found = [size - 1]
    while found[-1] > 1:
        found.append(found[-1] // 2)
    return found


def paired(terms, axis):
    hops = offsets(lax.axis_size(axis))
    parts = []
    for m, x in enumerate(terms):
        order = hops if m else hops[::-1]
        for step, offset in enumerate(order):
            y = swapped(x, axis, offset)
            if step + 1 < len(order):
                x = x + y
        parts.append((x, y))
    return parts


def gathered(odd, even):
    mine = even + swapped(odd, "shard", 1)
    terms = [mine[0]]
    for j in range(1, mine.shape[0]):
        terms.append(swapped(mine[j], "shard", 2 * j))
    return tree(terms)


def spread(share, half):
    terms = [share]
    for j in range(1, half):
        terms.append(swapped(share, "shard", 2 * j))
    return jnp.stack(terms)


def compress(ag, ae, wa, fg, fe, wf):
    plan = Plan((ag.shape[1], fg.shape[1]), (ag.shape[2], fg.shape[2]), wa.shape[0], lax.axis_size("shard"))
    scale = 1.0 / lax.axis_size("dp")
    *second, left_1 = load(plan, 1, (fg, fe, wf), True)
    *first, left_0 = load(plan, 0, (ag, ae, wa), False)
    matrix = first + second
    terms = [left_0, left_1]
    inverse = None
    for sweep in range(ITERS):
        parts = paired(terms, "dp")
        odd, even, whole = right(plan, parts, matrix, inverse, None if inverse is None else scale)
        joint = gathered(odd, even)
        inverse = factor(plan, joint[:, plan.share :])
        share = tree(exchanged(joint[:, : plan.share], "dp"))
        if sweep + 1 == ITERS:
            basis = basis_of(plan, inverse, whole)
            share, inverse, basis = lax.optimization_barrier((share, inverse, basis))
        else:
            share, inverse = lax.optimization_barrier((share, inverse))
        near = spread(share, plan.half)
        far = swapped(near, "shard", 1)
        if sweep + 1 < ITERS:
            terms = left(plan, near, far, matrix)
    return carry(plan, near, far, inverse, basis, matrix, scale)


def solution(mesh):
    tall = P("dp", "shard", None)
    return jax.shard_map(
        compress,
        mesh=mesh,
        in_specs=(tall, tall, P(), tall, tall, P()),
        out_specs=(tall, tall, P(), P()),
        check_vma=False,
    )
```
